32 devices in a mesh: batch: 4 (over y, x), dom: 8 (over z, core).
Axes of the slice: x: 2, y: 2, z: 4, core: 2. Of those that a mesh axis runs over, the one named last changes fastest.
Arguments:
- cell_feat: bfloat16 [4, 4096, 256], P('batch', 'dom'), may hold values from -6 to 6
- net_feat: bfloat16 [4, 4096, 256], P('batch', 'dom'), may hold values from -6 to 6
- net_grad: bfloat16 [4, 4096, 256], P('batch', 'dom'), may hold values from -6 to 6
- w_first: bfloat16 [512, 512], replicated, may hold values from -0.25 to 0.25
- w_second: bfloat16 [512, 256], replicated, may hold values from -0.25 to 0.25
- pin_cell: int32 [4, 8, 8, 256], P('batch', 'dom'), may hold values from 0 to 511
- pin_net: int32 [4, 8, 8, 256], P('batch', 'dom'), may hold values from 0 to 511
- pin_count: int32 [4, 8, 8], P('batch', 'dom'), may hold values from 224 to 256, as said below
Outputs:
- cell_out: float32 [4, 4096, 256], P('batch', 'dom')
- net_out: float32 [4, 4096, 256], P('batch', 'dom')
- first_total: float32 [512, 512], replicated
- second_total: float32 [512, 256], replicated
The draws below stay inside these ranges and needn't reach their ends.
Inputs may be any that keep to these rules, and one draw needn't show every extreme that they name: `pin_count`: every partition sends at most 256 live slots to each owner, and in every design each partition fills its slots to some owner.
All inputs are finite; a program needn't handle non-finite values.
Results may differ from the reference program's by a relative error of at most 0.004.
Values may be sent and summed in bfloat16 or wider, within the bound.
A program may use at most 64 MiB of HBM per device.

```python
import math
import jax
import jax.numpy as jnp
import numpy as np
from jax import lax

H = 256
IN = 512
MID = 512
SLOT_DEV = 2048
CAP = 256
CELL_DEV = 512
NET_DEV = 512
DESIGNS = 4
CELLS = 4096
NETS = 4096
N_DOM = 8


def draw_pin_count(key, part):
    base_key = jax.random.fold_in(key, 7)
    first_key, second_key = jax.random.split(base_key)
    lowest = CAP - max(1, CAP // 8)
    base = jax.random.randint(first_key, (DESIGNS, N_DOM, N_DOM), lowest, CAP + 1)
    picked = jax.random.randint(second_key, (DESIGNS, N_DOM, 1), 0, N_DOM)
    column = lax.broadcasted_iota(jnp.int32, (DESIGNS, N_DOM, N_DOM), 2)
    return jnp.where(column == picked, CAP, base).astype(jnp.int32)


def plant(values, own_key, least, high):
    index_at = [jax.random.randint(jax.random.fold_in(own_key, axis), (), 0, length) for axis, length in enumerate(values.shape)]
    main_axis = values.shape.index(max(values.shape))
    next_to = index_at[:main_axis] + [(index_at[main_axis] + 1) % values.shape[main_axis]] + index_at[main_axis + 1:]
    return values.at[tuple(index_at)].set(least).at[tuple(next_to)].set(high)


def block_levels(key, extent, cuts, smallest, top_value):
    def one(axis_at, blocks):
        steps = jax.random.uniform(jax.random.fold_in(jax.random.fold_in(key, 6), axis_at), (blocks,), jnp.float32, smallest / len(cuts), top_value / len(cuts))
        return jnp.repeat(jnp.exp(steps), extent[axis_at] // blocks).reshape((-1,) + (1,) * (len(extent) - axis_at - 1))

    gain = one(*cuts[0])
    for cut in cuts[1:]:
        gain = gain * one(*cut)
    return gain


def rank_bounds(number_of, lean):
    portions = [(1 << 20) // math.isqrt(rank ** lean) + 1 for rank in range(1, number_of + 1)]
    deviation = 1 + sum(portions) // (1 << 30)
    return np.cumsum(np.array([max(1, weight // deviation) for weight in portions]))


def ranked_ids(rng, dims, number_of, slope):
    listing = rank_bounds(number_of, slope)
    ticket = jax.random.randint(jax.random.fold_in(rng, 1), dims, 0, int(listing[number_of - 1]))
    grade = jnp.searchsorted(jnp.asarray(listing, jnp.int32), ticket, side="right")
    return jax.random.permutation(jax.random.fold_in(rng, 2), number_of)[grade].astype(jnp.int32)


def bell_draw(rng, dims, deviation, reach, pieces=(), kind=jnp.bfloat16):
    array = jax.random.normal(rng, dims, jnp.float32) * deviation
    if len(pieces) > 0:
        array = block_levels(rng, dims, pieces, -0.22, 0.18) * array
    return jnp.clip(array, min=-reach, max=reach).astype(kind)


def setup_inputs(seed: int = 0) -> dict:
    seeds = jax.random.split(jax.random.key(seed), 9)
    cell_feat = bell_draw(seeds[0], (DESIGNS, CELLS, H), 1.0, 6.0, ((0, 4), (1, 8)))
    net_feat = bell_draw(seeds[1], (DESIGNS, NETS, H), 1.0, 6.0, ((0, 4), (1, 8)))
    net_grad = bell_draw(seeds[2], (DESIGNS, NETS, H), 1.0, 6.0, ((0, 4), (1, 8)))
    w_first = bell_draw(seeds[3], (IN, MID), IN ** -0.5, 0.25)
    w_second = bell_draw(seeds[4], (MID, H), MID ** -0.5, 0.25)
    pin_cell = plant(jax.random.randint(seeds[5], (DESIGNS, N_DOM, N_DOM, CAP), 0, CELL_DEV), jax.random.fold_in(seeds[5], 1), 0, CELL_DEV - 1).astype(jnp.int32)
    pin_net = plant(ranked_ids(seeds[6], (DESIGNS, N_DOM, N_DOM, CAP), NET_DEV, 1), jax.random.fold_in(seeds[6], 3), 0, NET_DEV - 1).astype(jnp.int32)
    pin_count = draw_pin_count(jax.random.fold_in(seeds[8], 71), 0)
    return dict(cell_feat=cell_feat, net_feat=net_feat, net_grad=net_grad, w_first=w_first, w_second=w_second, pin_cell=pin_cell, pin_net=pin_net, pin_count=pin_count)


def backward_core(pin_input, pin_grad, w_first, w_second):
    pre_act = jnp.dot(pin_input, w_first, preferred_element_type=jnp.float32)
    hidden = jax.nn.silu(pre_act).astype(jnp.bfloat16)
    second_part = lax.dot_general(hidden, pin_grad, (((0,), (0,)), ((), ())), preferred_element_type=jnp.float32)
    hidden_grad = lax.dot_general(pin_grad, w_second, (((1,), (1,)), ((), ())), preferred_element_type=jnp.float32)
    gate_sig = jax.nn.sigmoid(pre_act)
    pre_grad = (hidden_grad * gate_sig * (1.0 + pre_act * (1.0 - gate_sig))).astype(jnp.bfloat16)
    first_part = lax.dot_general(pin_input, pre_grad, (((0,), (0,)), ((), ())), preferred_element_type=jnp.float32)
    input_grad = lax.dot_general(pre_grad, w_first, (((1,), (1,)), ((), ())), preferred_element_type=jnp.float32).astype(jnp.bfloat16)
    return (input_grad, first_part, second_part)

def reference(cell_feat, net_feat, net_grad, w_first, w_second, pin_cell, pin_net, pin_count):
    shape_slots = (N_DOM, N_DOM, CAP)
    source = lax.broadcasted_iota(jnp.int32, shape_slots, 0)
    owner = lax.broadcasted_iota(jnp.int32, shape_slots, 1)
    position = lax.broadcasted_iota(jnp.int32, shape_slots, 2)

    def per_design(carry, item):
        cell_table, net_table, grad_table, slot_cell, slot_net, counts = item
        is_live = (position < counts[:, :, None]).reshape(-1)
        cell_index = (source * CELL_DEV + slot_cell).reshape(-1).astype(jnp.int32)
        net_index = (owner * NET_DEV + slot_net).reshape(-1).astype(jnp.int32)
        pin_input = jnp.concatenate([jnp.take(cell_table, cell_index, axis=0), jnp.take(net_table, net_index, axis=0)], axis=1)
        pin_grad = jnp.where(is_live[:, None], jnp.take(grad_table, net_index, axis=0), jnp.zeros((), jnp.bfloat16))
        input_grad, first_part, second_part = backward_core(pin_input, pin_grad, w_first, w_second)
        cell_part = jax.ops.segment_sum(input_grad[:, :H].astype(jnp.float32), cell_index, num_segments=CELLS)
        net_part = jax.ops.segment_sum(input_grad[:, H:].astype(jnp.float32), net_index, num_segments=NETS)
        return ((carry[0] + first_part, carry[1] + second_part), (cell_part, net_part))
    start = (jnp.zeros((IN, MID), jnp.float32), jnp.zeros((MID, H), jnp.float32))
    sums, outs = lax.scan(per_design, start, (cell_feat, net_feat, net_grad, pin_cell, pin_net, pin_count))
    wgrad_scale = 1.0 / math.sqrt(DESIGNS * N_DOM * SLOT_DEV)
    return (outs[0], outs[1], sums[0] * wgrad_scale, sums[1] * wgrad_scale)
```

```python
import functools
import math

import jax
import jax.numpy as jnp
from jax import lax
from jax.experimental import pallas as pl
from jax.experimental.pallas import tpu as pltpu
from jax.sharding import PartitionSpec as P

BF = jnp.bfloat16
F32 = jnp.float32
MESH = pl.DeviceIdType.MESH


def mm(a, b):
    return jnp.dot(a, b, preferred_element_type=F32)


def mm_t(a, b):
    return lax.dot_general(a, b, (((1,), (1,)), ((), ())), preferred_element_type=F32)


def one_hot_t(row, count):
    at = lax.broadcasted_iota(jnp.int32, (count, row.shape[1]), 0)
    return jnp.where(at == row, 1.0, 0.0).astype(BF)


def kernel(
    batches, owners, rows_z, scale,
    cell, net, grad, w1, w2, slot_cell, code,
    cell_out, net_out, first_out, second_out,
    cell_t, net_t, w1_t, x_t, total,
    send, recv, code_recv, ret_send, ret_recv,
    core_send, core_recv, part_core, bat_send, bat_recv, part_bat, z_send, z_recv, full,
    send_sem, recv_sem, code_ssem, code_rsem, ret_ssem, ret_rsem,
    core_sem, bat_ssem, bat_rsem, z_ssem, z_rsem, gcore_sem, gbat_ssem, gbat_rsem, gz_ssem, gz_rsem,
):
    bat = lax.axis_index("batch")
    me = lax.axis_index("dom")
    feat = cell.shape[1]
    cells = cell.shape[0]
    nets = net.shape[0]
    mid = w1.shape[1]
    core = lax.rem(me, 2)
    depth = owners // 2
    zat = me // 2
    sibling = me + 1 - 2 * core
    half = total.shape[0] // 2

    barrier = pltpu.get_barrier_semaphore()

    def greet_dom(k, carry):
        pl.semaphore_signal(
            barrier, inc=1, device_id=(bat, lax.rem(me + k, owners)), device_id_type=MESH
        )
        return carry

    def greet_batch(k, carry):
        pl.semaphore_signal(
            barrier, inc=1, device_id=(lax.rem(bat + k, batches), me), device_id_type=MESH
        )
        return carry

    lax.fori_loop(1, owners, greet_dom, 0)
    lax.fori_loop(1, batches, greet_batch, 0)

    cell_t[...] = cell[...].T
    code_recv[me] = code[me]
    recv[me] = mm(cell_t[...], one_hot_t(slot_cell[me, 0:1, :], cells)).astype(BF)

    pl.semaphore_wait(barrier, owners + batches - 2)

    def code_copy(to, frm):
        return pltpu.make_async_remote_copy(
            src_ref=code.at[to], dst_ref=code_recv.at[frm],
            send_sem=code_ssem.at[to], recv_sem=code_rsem.at[frm],
            device_id=(bat, to), device_id_type=MESH,
        )

    def row_copy(to, frm):
        return pltpu.make_async_remote_copy(
            src_ref=send.at[to], dst_ref=recv.at[frm],
            send_sem=send_sem.at[to], recv_sem=recv_sem.at[frm],
            device_id=(bat, to), device_id_type=MESH,
        )

    def ret_copy(to, frm):
        return pltpu.make_async_remote_copy(
            src_ref=ret_send.at[to], dst_ref=ret_recv.at[frm],
            send_sem=ret_ssem.at[to], recv_sem=ret_rsem.at[frm],
            device_id=(bat, to), device_id_type=MESH,
        )

    def send_rows(k, carry):
        to = lax.rem(me + k, owners)
        code_copy(to, me).start()
        send[to] = mm(cell_t[...], one_hot_t(slot_cell[to, 0:1, :], cells)).astype(BF)
        row_copy(to, me).start()
        return carry

    lax.fori_loop(1, owners, send_rows, 0)

    net_t[0:feat, :] = net[...].T
    net_t[feat:, :] = grad[...].T
    w1_t[...] = w1[...].T
    net_out[...] = jnp.zeros_like(net_out)
    total[...] = jnp.zeros_like(total)

    def work(src):
        hot = one_hot_t(code_recv[src, 0:1, :], nets)
        rows = mm(net_t[...], hot).astype(BF)
        x_t[0:feat, :] = recv[src]
        x_t[feat:, :] = rows[0:feat, :]
        pin_grad = rows[feat:, :]
        pre = mm(w1_t[...], x_t[...])
        hidden_grad = mm(w2[...], pin_grad)
        sig = jax.nn.sigmoid(pre)
        hidden = (pre * sig).astype(BF)
        pre_grad = (hidden_grad * sig * (1.0 + pre * (1.0 - sig))).astype(BF)
        total[:, 0:mid] += mm_t(x_t[...], pre_grad)
        total[:, mid:] += mm_t(hidden, pin_grad)
        back = mm(w1[...], pre_grad).astype(BF)
        net_out[...] += mm_t(hot, back[feat:, :])
        return back[0:feat, :]

    ret_recv[me] = work(me)

    def step(k, carry):
        src = lax.rem(me - k + owners, owners)
        code_copy(src, src).wait_recv()
        row_copy(src, src).wait_recv()
        ret_send[src] = work(src)
        ret_copy(src, me).start()
        return carry

    lax.fori_loop(1, owners, step, 0)

    core_send[...] = total[pl.ds(pl.multiple_of((1 - core) * half, half), half), :].astype(BF)
    core_copy = pltpu.make_async_remote_copy(
        src_ref=core_send, dst_ref=core_recv, send_sem=core_sem.at[0], recv_sem=core_sem.at[1],
        device_id=(bat, sibling), device_id_type=MESH,
    )
    core_copy.start()
    core_copy.wait()
    mine = total[pl.ds(pl.multiple_of(core * half, half), half), :] + core_recv[...].astype(F32)
    part_core[...] = mine.reshape(part_core.shape)
    bat_send[...] = mine.astype(BF).reshape(bat_send.shape)

    def bat_copy(to, frm):
        return pltpu.make_async_remote_copy(
            src_ref=bat_send.at[to], dst_ref=bat_recv.at[frm],
            send_sem=bat_ssem.at[to], recv_sem=bat_rsem.at[frm],
            device_id=(to, me), device_id_type=MESH,
        )

    def bat_go(k, carry):
        bat_copy(lax.rem(bat + k, batches), bat).start()
        return carry

    lax.fori_loop(1, batches, bat_go, 0)
    part_bat[...] = part_core[bat]

    def bat_add(k, carry):
        frm = lax.rem(bat - k + batches, batches)
        bat_copy(frm, frm).wait_recv()
        part_bat[...] += bat_recv[frm].astype(F32)
        return carry

    lax.fori_loop(1, batches, bat_add, 0)
    split_z = z_send.shape[0] > 1
    z_send[...] = part_bat[...].astype(BF).reshape(z_send.shape)

    def z_copy(to, frm):
        return pltpu.make_async_remote_copy(
            src_ref=z_send.at[to if split_z else 0], dst_ref=z_recv.at[frm],
            send_sem=z_ssem.at[to], recv_sem=z_rsem.at[frm],
            device_id=(bat, 2 * to + core), device_id_type=MESH,
        )

    def z_go(k, carry):
        z_copy(lax.rem(zat + k, depth), zat).start()
        return carry

    lax.fori_loop(1, depth, z_go, 0)
    z_recv[zat] = z_send[zat if split_z else 0]

    def z_wait(k, carry):
        frm = lax.rem(zat - k + depth, depth)
        z_copy(frm, frm).wait_recv()
        return carry

    lax.fori_loop(1, depth, z_wait, 0)
    summed = z_recv[0].astype(F32)
    for other in range(1, depth):
        summed += z_recv[other].astype(F32)
    summed = summed.astype(BF)

    def gz_copy(to, frm):
        spot = full.at[core, bat, pl.ds(frm * rows_z, rows_z), :]
        return pltpu.make_async_remote_copy(
            src_ref=spot, dst_ref=spot,
            send_sem=gz_ssem.at[to], recv_sem=gz_rsem.at[frm],
            device_id=(bat, 2 * to + core), device_id_type=MESH,
        )

    def gz_go(k, carry):
        gz_copy(lax.rem(zat + k, depth), zat).start()
        return carry

    def gz_wait(k, carry):
        frm = lax.rem(zat - k + depth, depth)
        gz_copy(frm, frm).wait_recv()
        return carry

    if split_z:
        full[core, bat, pl.ds(pl.multiple_of(zat * rows_z, rows_z), rows_z), :] = summed
        lax.fori_loop(1, depth, gz_go, 0)
        lax.fori_loop(1, depth, gz_wait, 0)
    else:
        full[core, bat] = summed

    def gbat_copy(to, frm):
        return pltpu.make_async_remote_copy(
            src_ref=full.at[core, frm], dst_ref=full.at[core, frm],
            send_sem=gbat_ssem.at[to], recv_sem=gbat_rsem.at[frm],
            device_id=(to, me), device_id_type=MESH,
        )

    def gbat_go(k, carry):
        gbat_copy(lax.rem(bat + k, batches), bat).start()
        return carry

    def gbat_wait(k, carry):
        frm = lax.rem(bat - k + batches, batches)
        gbat_copy(frm, frm).wait_recv()
        return carry

    lax.fori_loop(1, batches, gbat_go, 0)

    cell_out[...] = mm_t(one_hot_t(slot_cell[me, 0:1, :], cells), ret_recv[me])

    def gather_back(k, carry):
        frm = lax.rem(me + k, owners)
        ret_copy(frm, frm).wait_recv()
        cell_out[...] += mm_t(one_hot_t(slot_cell[frm, 0:1, :], cells), ret_recv[frm])
        return carry

    lax.fori_loop(1, owners, gather_back, 0)

    lax.fori_loop(1, batches, gbat_wait, 0)

    def gcore_copy(frm):
        return pltpu.make_async_remote_copy(
            src_ref=full.at[frm], dst_ref=full.at[frm],
            send_sem=gcore_sem.at[0], recv_sem=gcore_sem.at[1],
            device_id=(bat, sibling), device_id_type=MESH,
        )

    gcore_copy(core).start()
    gcore_copy(1 - core).wait_recv()
    whole = full[...].reshape(total.shape).astype(F32) * scale
    first_out[...] = whole[:, 0:mid]
    second_out[...] = whole[:, mid:]

    def drain_dom(k, carry):
        to = lax.rem(me + k, owners)
        code_copy(to, me).wait_send()
        row_copy(to, me).wait_send()
        ret_copy(to, me).wait_send()
        return carry

    def drain_batch(k, carry):
        to = lax.rem(bat + k, batches)
        bat_copy(to, bat).wait_send()
        gbat_copy(to, bat).wait_send()
        return carry

    def drain_z(k, carry):
        to = lax.rem(zat + k, depth)
        z_copy(to, zat).wait_send()
        if split_z:
            gz_copy(to, zat).wait_send()
        return carry

    lax.fori_loop(1, owners, drain_dom, 0)
    lax.fori_loop(1, batches, drain_batch, 0)
    lax.fori_loop(1, depth, drain_z, 0)
    gcore_copy(core).wait_send()


def on_device(cell_feat, net_feat, net_grad, w_first, w_second, pin_cell, pin_net, pin_count):
    owners = lax.axis_size("dom")
    batches = lax.axis_size("batch")
    cell, net, grad = cell_feat[0], net_feat[0], net_grad[0]
    capacity = pin_cell.shape[3]
    cells, feat = cell.shape
    nets = net.shape[0]
    fan_in, mid = w_first.shape
    width = mid + feat
    depth = owners // 2
    is_live = lax.broadcasted_iota(jnp.int32, (owners, capacity), 1) < pin_count[0, 0][:, None]
    code = jnp.where(is_live, pin_net[0, 0], -1)
    code = jnp.broadcast_to(code[:, None, :], (owners, 8, capacity))
    slot_cell = jnp.broadcast_to(pin_cell[0, 0][:, None, :], (owners, 8, capacity))
    scale = 1.0 / math.sqrt(batches * owners * owners * capacity)
    half = fan_in // 2
    rows_b = half // batches
    split_z = rows_b // depth >= 16
    rows_z = rows_b // depth if split_z else rows_b
    parts_z = depth if split_z else 1
    dma = pltpu.SemaphoreType.DMA
    vmem = pltpu.VMEM
    cell_out, net_out, first, second = pl.pallas_call(
        functools.partial(kernel, batches, owners, rows_z, scale),
        out_shape=(
            jax.ShapeDtypeStruct((cells, feat), F32),
            jax.ShapeDtypeStruct((nets, feat), F32),
            jax.ShapeDtypeStruct((fan_in, mid), F32),
            jax.ShapeDtypeStruct((mid, feat), F32),
        ),
        in_specs=[pl.BlockSpec(memory_space=pltpu.VMEM)] * 7,
        out_specs=[pl.BlockSpec(memory_space=pltpu.VMEM)] * 4,
        scratch_shapes=[
            vmem((feat, cells), BF),
            vmem((2 * feat, nets), BF),
            vmem((mid, fan_in), BF),
            vmem((fan_in, capacity), BF),
            vmem((fan_in, width), F32),
            vmem((owners, feat, capacity), BF),
            vmem((owners, feat, capacity), BF),
            vmem((owners, 8, capacity), jnp.int32),
            vmem((owners, feat, capacity), BF),
            vmem((owners, feat, capacity), BF),
            vmem((half, width), BF),
            vmem((half, width), BF),
            vmem((batches, rows_b, width), F32),
            vmem((batches, rows_b, width), BF),
            vmem((batches, rows_b, width), BF),
            vmem((rows_b, width), F32),
            vmem((parts_z, rows_z, width), BF),
            vmem((depth, rows_z, width), BF),
            vmem((2, batches, rows_b, width), BF),
            dma((owners,)), dma((owners,)), dma((owners,)), dma((owners,)),
            dma((owners,)), dma((owners,)),
            dma((2,)), dma((batches,)), dma((batches,)), dma((depth,)), dma((depth,)),
            dma((2,)), dma((batches,)), dma((batches,)), dma((depth,)), dma((depth,)),
        ],
        compiler_params=pltpu.CompilerParams(
            collective_id=0, has_side_effects=True, vmem_limit_bytes=48 * 1024 * 1024
        ),
    )(cell, net, grad, w_first, w_second, slot_cell, code)
    return (cell_out[None], net_out[None], first, second)


def solution(mesh):
    return jax.shard_map(
        on_device,
        mesh=mesh,
        in_specs=(
            P("batch", "dom", None),
            P("batch", "dom", None),
            P("batch", "dom", None),
            P(),
            P(),
            P("batch", "dom", None, None),
            P("batch", "dom", None, None),
            P("batch", "dom", None),
        ),
        out_specs=(P("batch", "dom", None), P("batch", "dom", None), P(), P()),
        check_vma=False,
    )
```

```python
import functools
import math

import jax
import jax.numpy as jnp
from jax import lax
from jax.experimental import pallas as pl
from jax.experimental.pallas import tpu as pltpu
from jax.sharding import PartitionSpec as P

BF = jnp.bfloat16
F32 = jnp.float32
MESH = pl.DeviceIdType.MESH


def mm(a, b):
    return jnp.dot(a, b, preferred_element_type=F32)


def mm_t(a, b):
    return lax.dot_general(a, b, (((1,), (1,)), ((), ())), preferred_element_type=F32)


def one_hot_t(row, count):
    at = lax.broadcasted_iota(jnp.int32, (count, row.shape[1]), 0)
    return jnp.where(at == row, 1.0, 0.0).astype(BF)


def kernel(
    batches, owners, rows_z,
    cell_hbm, net_hbm, grad_hbm, w1_hbm, w2_hbm, cell_pin_hbm, net_pin_hbm, count_hbm,
    cell_out, net_out, full,
    cell, net, grad, w1, w2, slot_cell, net_pin, count, code,
    cell_t, net_t, w1_t, x_t, g_t, hot, total,
    send, recv, code_recv, ret_send, ret_recv,
    core_send, core_recv, part_core, bat_send, bat_recv, part_bat, z_send, z_recv,
    load_sem,
    send_sem, recv_sem, code_ssem, code_rsem, ret_ssem, ret_rsem,
    core_sem, bat_ssem, bat_rsem, z_ssem, z_rsem, gcore_sem, gbat_ssem, gbat_rsem, gz_ssem, gz_rsem,
):
    bat = lax.axis_index("batch")
    me = lax.axis_index("dom")
    feat = cell.shape[1]
    cells = cell.shape[0]
    nets = net.shape[0]
    mid = w1.shape[1]
    core = lax.rem(me, 2)
    depth = owners // 2
    zat = me // 2
    sibling = me + 1 - 2 * core
    half = total.shape[0] // 2

    loads = [
        pltpu.make_async_copy(a, b, load_sem.at[i])
        for i, (a, b) in enumerate(
            (
                (cell_hbm, cell), (cell_pin_hbm, slot_cell), (net_pin_hbm, net_pin),
                (count_hbm, count), (net_hbm, net), (grad_hbm, grad), (w1_hbm, w1), (w2_hbm, w2),
            )
        )
    ]
    for load in loads:
        load.start()

    barrier = pltpu.get_barrier_semaphore()

    def greet_dom(k, carry):
        pl.semaphore_signal(
            barrier, inc=1, device_id=(bat, lax.rem(me + k, owners)), device_id_type=MESH
        )
        return carry

    def greet_batch(k, carry):
        pl.semaphore_signal(
            barrier, inc=1, device_id=(lax.rem(bat + k, batches), me), device_id_type=MESH
        )
        return carry

    lax.fori_loop(1, owners, greet_dom, 0)
    lax.fori_loop(1, batches, greet_batch, 0)

    for load in loads[:4]:
        load.wait()
    cell_t[...] = cell[...].T
    cap = code.shape[2]
    lane = lax.broadcasted_iota(jnp.int32, (8, cap), 1)

    def cell_hot(to):
        return one_hot_t(slot_cell[pl.ds(to, 1), :], cells)

    def net_code(to, carry):
        code[to] = jnp.where(lane < count[0, to], net_pin[pl.ds(to, 1), :], -1)
        return carry

    lax.fori_loop(0, owners, net_code, 0)
    code_recv[me] = code[me]
    recv[me] = mm(cell_t[...], cell_hot(me)).astype(BF)

    pl.semaphore_wait(barrier, owners + batches - 2)

    def code_copy(to, frm):
        return pltpu.make_async_remote_copy(
            src_ref=code.at[to], dst_ref=code_recv.at[frm],
            send_sem=code_ssem.at[to], recv_sem=code_rsem.at[frm],
            device_id=(bat, to), device_id_type=MESH,
        )

    def row_copy(to, frm):
        return pltpu.make_async_remote_copy(
            src_ref=send.at[to], dst_ref=recv.at[frm],
            send_sem=send_sem.at[to], recv_sem=recv_sem.at[frm],
            device_id=(bat, to), device_id_type=MESH,
        )

    def ret_copy(to, frm):
        return pltpu.make_async_remote_copy(
            src_ref=ret_send.at[to], dst_ref=ret_recv.at[frm],
            send_sem=ret_ssem.at[to], recv_sem=ret_rsem.at[frm],
            device_id=(bat, to), device_id_type=MESH,
        )

    def send_to(to):
        code_copy(to, me).start()
        send[to] = mm(cell_t[...], cell_hot(to)).astype(BF)
        row_copy(to, me).start()

    def send_rows(j, carry):
        chip = lax.rem(zat - j + depth, depth)
        for i in range(2):
            send_to(2 * chip + i)
        return carry

    send_to(sibling)
    lax.fori_loop(1, depth, send_rows, 0)

    for load in loads[4:]:
        load.wait()
    net_t[0:feat, :] = net[...].T
    net_t[feat:, :] = grad[...].T
    w1_t[...] = w1[...].T
    net_out[...] = jnp.zeros_like(net_out)
    total[...] = jnp.zeros_like(total)

    def step(j, carry):
        chip = lax.rem(zat + j, depth)
        for i in range(2):
            src = 2 * chip + i
            spot = pl.ds(i * cap, cap)

            @pl.when(src != me)
            def _():
                code_copy(src, src).wait_recv()
                row_copy(src, src).wait_recv()

            hot[:, spot] = one_hot_t(code_recv[src, 0:1, :], nets)
            x_t[0:feat, spot] = recv[src]
        rows = mm(net_t[...], hot[...]).astype(BF)
        x_t[feat:, :] = rows[0:feat, :]
        g_t[...] = rows[feat:, :]
        pre = mm(w1_t[...], x_t[...])
        hidden_grad = mm(w2[...], g_t[...])
        sig = 0.5 + 0.5 * jnp.tanh(0.5 * pre)
        hidden = (pre * sig).astype(BF)
        pre_grad = (hidden_grad * sig * (1.0 + pre * (1.0 - sig))).astype(BF)
        back = mm(w1[...], pre_grad).astype(BF)
        for i in range(2):
            src = 2 * chip + i
            ret_send[src] = back[0:feat, i * cap : (i + 1) * cap]

            @pl.when(src != me)
            def _():
                ret_copy(src, me).start()

        total[:, 0:mid] += mm_t(x_t[...], pre_grad)
        total[:, mid:] += mm_t(hidden, g_t[...])
        net_out[...] += mm_t(hot[...], back[feat:, :])
        return carry

    lax.fori_loop(0, depth, step, 0)

    core_send[...] = total[pl.ds(pl.multiple_of((1 - core) * half, half), half), :].astype(BF)
    core_copy = pltpu.make_async_remote_copy(
        src_ref=core_send, dst_ref=core_recv, send_sem=core_sem.at[0], recv_sem=core_sem.at[1],
        device_id=(bat, sibling), device_id_type=MESH,
    )
    core_copy.start()
    core_copy.wait()
    mine = total[pl.ds(pl.multiple_of(core * half, half), half), :] + core_recv[...].astype(F32)
    part_core[...] = mine.reshape(part_core.shape)
    bat_send[...] = mine.astype(BF).reshape(bat_send.shape)

    def bat_copy(to, frm):
        return pltpu.make_async_remote_copy(
            src_ref=bat_send.at[to], dst_ref=bat_recv.at[frm],
            send_sem=bat_ssem.at[to], recv_sem=bat_rsem.at[frm],
            device_id=(to, me), device_id_type=MESH,
        )

    def bat_go(k, carry):
        bat_copy(lax.rem(bat + k, batches), bat).start()
        return carry

    lax.fori_loop(1, batches, bat_go, 0)
    part_bat[...] = part_core[bat]

    def bat_add(k, carry):
        frm = lax.rem(bat - k + batches, batches)
        bat_copy(frm, frm).wait_recv()
        part_bat[...] += bat_recv[frm].astype(F32)
        return carry

    lax.fori_loop(1, batches, bat_add, 0)
    split_z = z_send.shape[0] > 1
    z_send[...] = part_bat[...].astype(BF).reshape(z_send.shape)

    def z_copy(to, frm):
        return pltpu.make_async_remote_copy(
            src_ref=z_send.at[to if split_z else 0], dst_ref=z_recv.at[frm],
            send_sem=z_ssem.at[to], recv_sem=z_rsem.at[frm],
            device_id=(bat, 2 * to + core), device_id_type=MESH,
        )

    def z_go(k, carry):
        z_copy(lax.rem(zat + k, depth), zat).start()
        return carry

    lax.fori_loop(1, depth, z_go, 0)
    z_recv[zat] = z_send[zat if split_z else 0]

    def z_wait(k, carry):
        frm = lax.rem(zat - k + depth, depth)
        z_copy(frm, frm).wait_recv()
        return carry

    lax.fori_loop(1, depth, z_wait, 0)
    summed = z_recv[0].astype(F32)
    for other in range(1, depth):
        summed += z_recv[other].astype(F32)
    summed = summed.astype(BF)

    def gz_copy(to, frm):
        spot = full.at[core, bat, pl.ds(frm * rows_z, rows_z), :]
        return pltpu.make_async_remote_copy(
            src_ref=spot, dst_ref=spot,
            send_sem=gz_ssem.at[to], recv_sem=gz_rsem.at[frm],
            device_id=(bat, 2 * to + core), device_id_type=MESH,
        )

    def gz_go(k, carry):
        gz_copy(lax.rem(zat + k, depth), zat).start()
        return carry

    def gz_wait(k, carry):
        frm = lax.rem(zat - k + depth, depth)
        gz_copy(frm, frm).wait_recv()
        return carry

    if split_z:
        full[core, bat, pl.ds(pl.multiple_of(zat * rows_z, rows_z), rows_z), :] = summed
        lax.fori_loop(1, depth, gz_go, 0)
        lax.fori_loop(1, depth, gz_wait, 0)
    else:
        full[core, bat] = summed

    def gbat_copy(to, frm):
        return pltpu.make_async_remote_copy(
            src_ref=full.at[core, frm], dst_ref=full.at[core, frm],
            send_sem=gbat_ssem.at[to], recv_sem=gbat_rsem.at[frm],
            device_id=(to, me), device_id_type=MESH,
        )

    def gbat_go(k, carry):
        gbat_copy(lax.rem(bat + k, batches), bat).start()
        return carry

    def gbat_wait(k, carry):
        frm = lax.rem(bat - k + batches, batches)
        gbat_copy(frm, frm).wait_recv()
        return carry

    lax.fori_loop(1, batches, gbat_go, 0)

    cell_out[...] = mm_t(cell_hot(me), ret_send[me])

    def gather_back(k, carry):
        frm = lax.rem(me + k, owners)
        ret_copy(frm, frm).wait_recv()
        cell_out[...] += mm_t(cell_hot(frm), ret_recv[frm])
        return carry

    lax.fori_loop(1, owners, gather_back, 0)

    lax.fori_loop(1, batches, gbat_wait, 0)

    def gcore_copy(frm):
        return pltpu.make_async_remote_copy(
            src_ref=full.at[frm], dst_ref=full.at[frm],
            send_sem=gcore_sem.at[0], recv_sem=gcore_sem.at[1],
            device_id=(bat, sibling), device_id_type=MESH,
        )

    gcore_copy(core).start()
    gcore_copy(1 - core).wait_recv()

    def drain_dom(k, carry):
        to = lax.rem(me + k, owners)
        code_copy(to, me).wait_send()
        row_copy(to, me).wait_send()
        ret_copy(to, me).wait_send()
        return carry

    def drain_batch(k, carry):
        to = lax.rem(bat + k, batches)
        bat_copy(to, bat).wait_send()
        gbat_copy(to, bat).wait_send()
        return carry

    def drain_z(k, carry):
        to = lax.rem(zat + k, depth)
        z_copy(to, zat).wait_send()
        if split_z:
            gz_copy(to, zat).wait_send()
        return carry

    lax.fori_loop(1, owners, drain_dom, 0)
    lax.fori_loop(1, batches, drain_batch, 0)
    lax.fori_loop(1, depth, drain_z, 0)
    gcore_copy(core).wait_send()


def finish(
    scale, cell_sum, net_sum, full, cell_out, net_out, first_out, second_out,
    held, first, second, sem,
):
    take = pltpu.make_async_copy(full, held, sem.at[4])
    take.start()
    copies = [
        pltpu.make_async_copy(a, b, sem.at[i])
        for i, (a, b) in enumerate(
            (
                (cell_sum, cell_out), (net_sum, net_out),
                (first, first_out), (second, second_out),
            )
        )
    ]
    copies[0].start()
    copies[1].start()
    mid = first.shape[1]
    take.wait()
    first[...] = held[:, 0:mid].astype(F32) * scale
    copies[2].start()
    second[...] = held[:, mid:].astype(F32) * scale
    copies[3].start()
    for copy in copies:
        copy.wait()


def on_device(cell_feat, net_feat, net_grad, w_first, w_second, pin_cell, pin_net, pin_count):
    owners = lax.axis_size("dom")
    batches = lax.axis_size("batch")
    cell, net, grad = cell_feat[0], net_feat[0], net_grad[0]
    capacity = pin_cell.shape[3]
    cells, feat = cell.shape
    nets = net.shape[0]
    fan_in, mid = w_first.shape
    width = mid + feat
    depth = owners // 2
    scale = 1.0 / math.sqrt(batches * owners * owners * capacity)
    half = fan_in // 2
    rows_b = half // batches
    split_z = rows_b // depth >= 16
    rows_z = rows_b // depth if split_z else rows_b
    parts_z = depth if split_z else 1
    dma = pltpu.SemaphoreType.DMA
    vmem = pltpu.VMEM
    hbm = pl.BlockSpec(memory_space=pltpu.HBM)
    on_chip = pl.BlockSpec(memory_space=pltpu.VMEM)
    cell_sum, net_sum, full = pl.pallas_call(
        functools.partial(kernel, batches, owners, rows_z),
        out_shape=(
            jax.ShapeDtypeStruct((cells, feat), F32),
            jax.ShapeDtypeStruct((nets, feat), F32),
            jax.ShapeDtypeStruct((2, batches, rows_b, width), BF),
        ),
        in_specs=[hbm] * 8,
        out_specs=[on_chip] * 3,
        scratch_shapes=[
            vmem((cells, feat), BF),
            vmem((nets, feat), BF),
            vmem((nets, feat), BF),
            vmem((fan_in, mid), BF),
            vmem((mid, feat), BF),
            vmem((owners, capacity), jnp.int32),
            vmem((owners, capacity), jnp.int32),
            pltpu.SMEM((1, owners), jnp.int32),
            vmem((owners, 8, capacity), jnp.int32),
            vmem((feat, cells), BF),
            vmem((2 * feat, nets), BF),
            vmem((mid, fan_in), BF),
            vmem((fan_in, 2 * capacity), BF),
            vmem((feat, 2 * capacity), BF),
            vmem((nets, 2 * capacity), BF),
            vmem((fan_in, width), F32),
            vmem((owners, feat, capacity), BF),
            vmem((owners, feat, capacity), BF),
            vmem((owners, 8, capacity), jnp.int32),
            vmem((owners, feat, capacity), BF),
            vmem((owners, feat, capacity), BF),
            vmem((half, width), BF),
            vmem((half, width), BF),
            vmem((batches, rows_b, width), F32),
            vmem((batches, rows_b, width), BF),
            vmem((batches, rows_b, width), BF),
            vmem((rows_b, width), F32),
            vmem((parts_z, rows_z, width), BF),
            vmem((depth, rows_z, width), BF),
            dma((8,)),
            dma((owners,)), dma((owners,)), dma((owners,)), dma((owners,)),
            dma((owners,)), dma((owners,)),
            dma((2,)), dma((batches,)), dma((batches,)), dma((depth,)), dma((depth,)),
            dma((2,)), dma((batches,)), dma((batches,)), dma((depth,)), dma((depth,)),
        ],
        compiler_params=pltpu.CompilerParams(
            collective_id=0, has_side_effects=True, vmem_limit_bytes=60 * 1024 * 1024
        ),
    )(cell, net, grad, w_first, w_second, pin_cell[0, 0], pin_net[0, 0], pin_count[0])
    cell_out, net_out, first, second = pl.pallas_call(
        functools.partial(finish, scale),
        out_shape=(
            jax.ShapeDtypeStruct((cells, feat), F32),
            jax.ShapeDtypeStruct((nets, feat), F32),
            jax.ShapeDtypeStruct((fan_in, mid), F32),
            jax.ShapeDtypeStruct((mid, feat), F32),
        ),
        in_specs=[hbm] * 3,
        out_specs=[hbm] * 4,
        scratch_shapes=[vmem((fan_in, width), BF), vmem((fan_in, mid), F32), vmem((mid, feat), F32), dma((5,))],
    )(cell_sum, net_sum, full.reshape(fan_in, width))
    return (cell_out[None], net_out[None], first, second)


def solution(mesh):
    return jax.shard_map(
        on_device,
        mesh=mesh,
        in_specs=(
            P("batch", "dom", None),
            P("batch", "dom", None),
            P("batch", "dom", None),
            P(),
            P(),
            P("batch", "dom", None, None),
            P("batch", "dom", None, None),
            P("batch", "dom", None),
        ),
        out_specs=(P("batch", "dom", None), P("batch", "dom", None), P(), P()),
        check_vma=False,
    )
```

```python
import functools
import math

import jax
import jax.numpy as jnp
from jax import lax
from jax.experimental import pallas as pl
from jax.experimental.pallas import tpu as pltpu
from jax.sharding import PartitionSpec as P

BF = jnp.bfloat16
F32 = jnp.float32
MESH = pl.DeviceIdType.MESH


def mm(a, b):
    return jnp.dot(a, b, preferred_element_type=F32)


def mm_t(a, b):
    return lax.dot_general(a, b, (((1,), (1,)), ((), ())), preferred_element_type=F32)


def one_hot_t(row, count):
    at = lax.broadcasted_iota(jnp.int32, (count, row.shape[1]), 0)
    return jnp.where(at == row, 1.0, 0.0).astype(BF)


def kernel(
    batches, owners, rows_z,
    cell_hbm, net_hbm, grad_hbm, w1_hbm, w2_hbm, cell_pin_hbm, net_pin_hbm, count_hbm,
    cell_out, net_out, full,
    cell, net, grad, w1, w2, slot_cell, net_pin, count, code,
    cell_t, net_t, w1_t, cell_all, net_all, grad_all, hot_all, pre_all, hid_grad_all, pre_grad_all, total,
    send, recv, code_recv, ret_send, ret_recv,
    core_send, core_recv, part_core, bat_send, bat_recv, part_bat, z_send, z_recv,
    load_sem,
    send_sem, recv_sem, code_ssem, code_rsem, ret_ssem, ret_rsem,
    core_sem, bat_ssem, bat_rsem, z_ssem, z_rsem, gcore_sem, gbat_ssem, gbat_rsem, gz_ssem, gz_rsem,
):
    bat = lax.axis_index("batch")
    me = lax.axis_index("dom")
    feat = cell.shape[1]
    cells = cell.shape[0]
    nets = net.shape[0]
    mid = w1.shape[1]
    core = lax.rem(me, 2)
    depth = owners // 2
    zat = me // 2
    sibling = me + 1 - 2 * core
    half = total.shape[0] // 2

    loads = [
        pltpu.make_async_copy(a, b, load_sem.at[i])
        for i, (a, b) in enumerate(
            (
                (cell_hbm, cell), (cell_pin_hbm, slot_cell), (net_pin_hbm, net_pin),
                (count_hbm, count), (net_hbm, net), (grad_hbm, grad), (w1_hbm, w1), (w2_hbm, w2),
            )
        )
    ]
    for load in loads:
        load.start()

    barrier = pltpu.get_barrier_semaphore()

    def greet_dom(k, carry):
        pl.semaphore_signal(
            barrier, inc=1, device_id=(bat, lax.rem(me + k, owners)), device_id_type=MESH
        )
        return carry

    def greet_batch(k, carry):
        pl.semaphore_signal(
            barrier, inc=1, device_id=(lax.rem(bat + k, batches), me), device_id_type=MESH
        )
        return carry

    lax.fori_loop(1, owners, greet_dom, 0)
    lax.fori_loop(1, batches, greet_batch, 0)

    for load in loads[:4]:
        load.wait()
    cell_t[...] = cell[...].T
    cap = code.shape[2]
    lane = lax.broadcasted_iota(jnp.int32, (8, cap), 1)

    def cell_hot(to):
        return one_hot_t(slot_cell[pl.ds(to, 1), :], cells)

    def net_code(to, carry):
        code[to] = jnp.where(lane < count[0, to], net_pin[pl.ds(to, 1), :], -1)
        return carry

    lax.fori_loop(0, owners, net_code, 0)
    code_recv[me] = code[me]
    recv[me] = mm(cell_t[...], cell_hot(me)).astype(BF)

    pl.semaphore_wait(barrier, owners + batches - 2)

    def code_copy(to, frm):
        return pltpu.make_async_remote_copy(
            src_ref=code.at[to], dst_ref=code_recv.at[frm],
            send_sem=code_ssem.at[to], recv_sem=code_rsem.at[frm],
            device_id=(bat, to), device_id_type=MESH,
        )

    def row_copy(to, frm):
        return pltpu.make_async_remote_copy(
            src_ref=send.at[to], dst_ref=recv.at[frm],
            send_sem=send_sem.at[to], recv_sem=recv_sem.at[frm],
            device_id=(bat, to), device_id_type=MESH,
        )

    def ret_copy(to, frm):
        return pltpu.make_async_remote_copy(
            src_ref=ret_send.at[to], dst_ref=ret_recv.at[frm],
            send_sem=ret_ssem.at[to], recv_sem=ret_rsem.at[frm],
            device_id=(bat, to), device_id_type=MESH,
        )

    def send_to(to):
        send[to] = mm(cell_t[...], cell_hot(to)).astype(BF)
        row_copy(to, me).start()

    def send_rows(j, carry):
        chip = lax.rem(zat - j + depth, depth)
        for i in range(2):
            send_to(2 * chip + i)
        return carry

    def send_codes(k, carry):
        code_copy(lax.rem(me + k, owners), me).start()
        return carry

    lax.fori_loop(1, owners, send_codes, 0)
    send_to(sibling)
    lax.fori_loop(1, depth, send_rows, 0)

    for load in loads[4:]:
        load.wait()
    net_t[0:feat, :] = net[...].T
    net_t[feat:, :] = grad[...].T
    w1_t[...] = w1[...].T
    total[...] = jnp.zeros_like(total)

    def early(j, carry):
        chip = lax.rem(zat + j, depth)
        for i in range(2):
            src = 2 * chip + i

            @pl.when(src != me)
            def _():
                code_copy(src, src).wait_recv()

            hot_all[j, :, i * cap : (i + 1) * cap] = one_hot_t(code_recv[src, 0:1, :], nets)
        rows = mm(net_t[...], hot_all[j]).astype(BF)
        net_all[j] = rows[0:feat, :]
        grad_all[j] = rows[feat:, :]
        pre_all[j] = mm(w1_t[:, feat:], net_all[j])
        hid_grad_all[j] = mm(w2[...], grad_all[j])
        return carry

    lax.fori_loop(0, depth, early, 0)

    def late(j, carry):
        chip = lax.rem(zat + j, depth)
        for i in range(2):
            src = 2 * chip + i

            @pl.when(src != me)
            def _():
                row_copy(src, src).wait_recv()

            cell_all[j, :, i * cap : (i + 1) * cap] = recv[src]
        pre = pre_all[j] + mm(w1_t[:, 0:feat], cell_all[j])
        sig = 0.5 + 0.5 * jnp.tanh(0.5 * pre)
        hidden = (pre * sig).astype(BF)
        pre_grad = (hid_grad_all[j] * sig * (1.0 + pre * (1.0 - sig))).astype(BF)
        pre_grad_all[j] = pre_grad
        back = mm(w1[0:feat, :], pre_grad).astype(BF)
        for i in range(2):
            src = 2 * chip + i
            ret_send[src] = back[:, i * cap : (i + 1) * cap]

            @pl.when(src != me)
            def _():
                ret_copy(src, me).start()

        total[0:feat, 0:mid] += mm_t(cell_all[j], pre_grad)
        total[feat:, 0:mid] += mm_t(net_all[j], pre_grad)
        total[:, mid:] += mm_t(hidden, grad_all[j])
        return carry

    lax.fori_loop(0, depth, late, 0)

    core_send[...] = total[pl.ds(pl.multiple_of((1 - core) * half, half), half), :].astype(BF)
    core_copy = pltpu.make_async_remote_copy(
        src_ref=core_send, dst_ref=core_recv, send_sem=core_sem.at[0], recv_sem=core_sem.at[1],
        device_id=(bat, sibling), device_id_type=MESH,
    )
    core_copy.start()
    net_out[...] = jnp.zeros_like(net_out)

    def net_side(j, carry):
        back = mm(w1[feat:, :], pre_grad_all[j]).astype(BF)
        net_out[...] += mm_t(hot_all[j], back)
        return carry

    lax.fori_loop(0, depth, net_side, 0)
    core_copy.wait()
    mine = total[pl.ds(pl.multiple_of(core * half, half), half), :] + core_recv[...].astype(F32)
    part_core[...] = mine.reshape(part_core.shape)
    bat_send[...] = mine.astype(BF).reshape(bat_send.shape)

    def bat_copy(to, frm):
        return pltpu.make_async_remote_copy(
            src_ref=bat_send.at[to], dst_ref=bat_recv.at[frm],
            send_sem=bat_ssem.at[to], recv_sem=bat_rsem.at[frm],
            device_id=(to, me), device_id_type=MESH,
        )

    def bat_go(k, carry):
        bat_copy(lax.rem(bat + k, batches), bat).start()
        return carry

    lax.fori_loop(1, batches, bat_go, 0)
    part_bat[...] = part_core[bat]

    def bat_add(k, carry):
        frm = lax.rem(bat - k + batches, batches)
        bat_copy(frm, frm).wait_recv()
        part_bat[...] += bat_recv[frm].astype(F32)
        return carry

    lax.fori_loop(1, batches, bat_add, 0)
    split_z = z_send.shape[0] > 1
    z_send[...] = part_bat[...].astype(BF).reshape(z_send.shape)

    def z_copy(to, frm):
        return pltpu.make_async_remote_copy(
            src_ref=z_send.at[to if split_z else 0], dst_ref=z_recv.at[frm],
            send_sem=z_ssem.at[to], recv_sem=z_rsem.at[frm],
            device_id=(bat, 2 * to + core), device_id_type=MESH,
        )

    def z_go(k, carry):
        z_copy(lax.rem(zat + k, depth), zat).start()
        return carry

    lax.fori_loop(1, depth, z_go, 0)
    z_recv[zat] = z_send[zat if split_z else 0]

    def z_wait(k, carry):
        frm = lax.rem(zat - k + depth, depth)
        z_copy(frm, frm).wait_recv()
        return carry

    lax.fori_loop(1, depth, z_wait, 0)
    summed = z_recv[0].astype(F32)
    for other in range(1, depth):
        summed += z_recv[other].astype(F32)
    summed = summed.astype(BF)

    def gz_copy(to, frm):
        spot = full.at[core, bat, pl.ds(frm * rows_z, rows_z), :]
        return pltpu.make_async_remote_copy(
            src_ref=spot, dst_ref=spot,
            send_sem=gz_ssem.at[to], recv_sem=gz_rsem.at[frm],
            device_id=(bat, 2 * to + core), device_id_type=MESH,
        )

    def gz_go(k, carry):
        gz_copy(lax.rem(zat + k, depth), zat).start()
        return carry

    def gz_wait(k, carry):
        frm = lax.rem(zat - k + depth, depth)
        gz_copy(frm, frm).wait_recv()
        return carry

    if split_z:
        full[core, bat, pl.ds(pl.multiple_of(zat * rows_z, rows_z), rows_z), :] = summed
        lax.fori_loop(1, depth, gz_go, 0)
        lax.fori_loop(1, depth, gz_wait, 0)
    else:
        full[core, bat] = summed

    def gbat_copy(to, frm):
        return pltpu.make_async_remote_copy(
            src_ref=full.at[core, frm], dst_ref=full.at[core, frm],
            send_sem=gbat_ssem.at[to], recv_sem=gbat_rsem.at[frm],
            device_id=(to, me), device_id_type=MESH,
        )

    def gbat_go(k, carry):
        gbat_copy(lax.rem(bat + k, batches), bat).start()
        return carry

    def gbat_wait(k, carry):
        frm = lax.rem(bat - k + batches, batches)
        gbat_copy(frm, frm).wait_recv()
        return carry

    lax.fori_loop(1, batches, gbat_go, 0)

    lax.fori_loop(1, batches, gbat_wait, 0)

    def gcore_copy(frm):
        return pltpu.make_async_remote_copy(
            src_ref=full.at[frm], dst_ref=full.at[frm],
            send_sem=gcore_sem.at[0], recv_sem=gcore_sem.at[1],
            device_id=(bat, sibling), device_id_type=MESH,
        )

    gcore_copy(core).start()

    cell_out[...] = mm_t(cell_hot(me), ret_send[me])

    def gather_back(k, carry):
        frm = lax.rem(me + k, owners)
        ret_copy(frm, frm).wait_recv()
        cell_out[...] += mm_t(cell_hot(frm), ret_recv[frm])
        return carry

    lax.fori_loop(1, owners, gather_back, 0)

    gcore_copy(1 - core).wait_recv()

    def drain_dom(k, carry):
        to = lax.rem(me + k, owners)
        code_copy(to, me).wait_send()
        row_copy(to, me).wait_send()
        ret_copy(to, me).wait_send()
        return carry

    def drain_batch(k, carry):
        to = lax.rem(bat + k, batches)
        bat_copy(to, bat).wait_send()
        gbat_copy(to, bat).wait_send()
        return carry

    def drain_z(k, carry):
        to = lax.rem(zat + k, depth)
        z_copy(to, zat).wait_send()
        if split_z:
            gz_copy(to, zat).wait_send()
        return carry

    lax.fori_loop(1, owners, drain_dom, 0)
    lax.fori_loop(1, batches, drain_batch, 0)
    lax.fori_loop(1, depth, drain_z, 0)
    gcore_copy(core).wait_send()


def finish(scale, cell_sum, net_sum, full, cell_out, net_out, first, second):
    mid = first.shape[1]
    cell_out[...] = cell_sum[...]
    net_out[...] = net_sum[...]
    first[...] = full[:, 0:mid].astype(F32) * scale
    second[...] = full[:, mid:].astype(F32) * scale


def on_device(cell_feat, net_feat, net_grad, w_first, w_second, pin_cell, pin_net, pin_count):
    owners = lax.axis_size("dom")
    batches = lax.axis_size("batch")
    cell, net, grad = cell_feat[0], net_feat[0], net_grad[0]
    capacity = pin_cell.shape[3]
    cells, feat = cell.shape
    nets = net.shape[0]
    fan_in, mid = w_first.shape
    width = mid + feat
    depth = owners // 2
    scale = 1.0 / math.sqrt(batches * owners * owners * capacity)
    half = fan_in // 2
    rows_b = half // batches
    split_z = rows_b // depth >= 16
    rows_z = rows_b // depth if split_z else rows_b
    parts_z = depth if split_z else 1
    dma = pltpu.SemaphoreType.DMA
    vmem = pltpu.VMEM
    hbm = pl.BlockSpec(memory_space=pltpu.HBM)
    on_chip = pl.BlockSpec(memory_space=pltpu.VMEM)

    def block(rows, columns):
        return pl.BlockSpec((rows // 4, columns), lambda i: (i, 0))

    cell_sum, net_sum, full = pl.pallas_call(
        functools.partial(kernel, batches, owners, rows_z),
        out_shape=(
            jax.ShapeDtypeStruct((cells, feat), F32),
            jax.ShapeDtypeStruct((nets, feat), F32),
            jax.ShapeDtypeStruct((2, batches, rows_b, width), BF),
        ),
        in_specs=[hbm] * 8,
        out_specs=[on_chip] * 3,
        scratch_shapes=[
            vmem((cells, feat), BF),
            vmem((nets, feat), BF),
            vmem((nets, feat), BF),
            vmem((fan_in, mid), BF),
            vmem((mid, feat), BF),
            vmem((owners, capacity), jnp.int32),
            vmem((owners, capacity), jnp.int32),
            pltpu.SMEM((1, owners), jnp.int32),
            vmem((owners, 8, capacity), jnp.int32),
            vmem((feat, cells), BF),
            vmem((2 * feat, nets), BF),
            vmem((mid, fan_in), BF),
            vmem((depth, feat, 2 * capacity), BF),
            vmem((depth, feat, 2 * capacity), BF),
            vmem((depth, feat, 2 * capacity), BF),
            vmem((depth, nets, 2 * capacity), BF),
            vmem((depth, mid, 2 * capacity), F32),
            vmem((depth, mid, 2 * capacity), F32),
            vmem((depth, mid, 2 * capacity), BF),
            vmem((fan_in, width), F32),
            vmem((owners, feat, capacity), BF),
            vmem((owners, feat, capacity), BF),
            vmem((owners, 8, capacity), jnp.int32),
            vmem((owners, feat, capacity), BF),
            vmem((owners, feat, capacity), BF),
            vmem((half, width), BF),
            vmem((half, width), BF),
            vmem((batches, rows_b, width), F32),
            vmem((batches, rows_b, width), BF),
            vmem((batches, rows_b, width), BF),
            vmem((rows_b, width), F32),
            vmem((parts_z, rows_z, width), BF),
            vmem((depth, rows_z, width), BF),
            dma((8,)),
            dma((owners,)), dma((owners,)), dma((owners,)), dma((owners,)),
            dma((owners,)), dma((owners,)),
            dma((2,)), dma((batches,)), dma((batches,)), dma((depth,)), dma((depth,)),
            dma((2,)), dma((batches,)), dma((batches,)), dma((depth,)), dma((depth,)),
        ],
        compiler_params=pltpu.CompilerParams(
            collective_id=0, has_side_effects=True, vmem_limit_bytes=60 * 1024 * 1024
        ),
    )(cell, net, grad, w_first, w_second, pin_cell[0, 0], pin_net[0, 0], pin_count[0])
    cell_out, net_out, first, second = pl.pallas_call(
        functools.partial(finish, scale),
        out_shape=(
            jax.ShapeDtypeStruct((cells, feat), F32),
            jax.ShapeDtypeStruct((nets, feat), F32),
            jax.ShapeDtypeStruct((fan_in, mid), F32),
            jax.ShapeDtypeStruct((mid, feat), F32),
        ),
        grid=(4,),
        in_specs=[block(cells, feat), block(nets, feat), block(fan_in, width)],
        out_specs=[block(cells, feat), block(nets, feat), block(fan_in, mid), block(mid, feat)],
    )(cell_sum, net_sum, full.reshape(fan_in, width))
    return (cell_out[None], net_out[None], first, second)


def solution(mesh):
    return jax.shard_map(
        on_device,
        mesh=mesh,
        in_specs=(
            P("batch", "dom", None),
            P("batch", "dom", None),
            P("batch", "dom", None),
            P(),
            P(),
            P("batch", "dom", None, None),
            P("batch", "dom", None, None),
            P("batch", "dom", None),
        ),
        out_specs=(P("batch", "dom", None), P("batch", "dom", None), P(), P()),
        check_vma=False,
    )
```

```python
import functools
import math

import jax
import jax.numpy as jnp
from jax import lax
from jax.experimental import pallas as pl
from jax.experimental.pallas import tpu as pltpu
from jax.sharding import PartitionSpec as P

BF = jnp.bfloat16
F32 = jnp.float32
MESH = pl.DeviceIdType.MESH


def mm(a, b):
    return jnp.dot(a, b, preferred_element_type=F32)


def mm_t(a, b):
    return lax.dot_general(a, b, (((1,), (1,)), ((), ())), preferred_element_type=F32)


def one_hot_t(row, count):
    at = lax.broadcasted_iota(jnp.int32, (count, row.shape[1]), 0)
    return jnp.where(at == row, 1.0, 0.0).astype(BF)


def kernel(
    batches, owners, rows_z,
    cell_hbm, net_hbm, grad_hbm, w1_hbm, w2_hbm, cell_pin_hbm, net_pin_hbm, count_hbm,
    cell_out, net_out, full,
    cell, net, grad, w1, w2, slot_cell, net_pin, count, code,
    cell_t, net_t, w1_t, cell_all, net_all, grad_all, hot_all, pre_all, hid_grad_all, pre_grad_all, total,
    send, recv, code_recv, ret_send, ret_recv,
    core_send, core_recv, bat_send, bat_recv, part_bat, z_send, z_recv,
    load_sem,
    send_sem, recv_sem, code_ssem, code_rsem, ret_ssem, ret_rsem,
    core_ssem, core_rsem, bat_ssem, bat_rsem, z_ssem, z_rsem, gcore_ssem, gcore_rsem, gbat_ssem, gbat_rsem, gz_ssem, gz_rsem,
):
    bat = lax.axis_index("batch")
    me = lax.axis_index("dom")
    feat = cell.shape[1]
    cells = cell.shape[0]
    nets = net.shape[0]
    mid = w1.shape[1]
    core = lax.rem(me, 2)
    depth = owners // 2
    zat = me // 2
    sibling = me + 1 - 2 * core
    half = total.shape[0] // 2

    loads = [
        pltpu.make_async_copy(a, b, load_sem.at[i])
        for i, (a, b) in enumerate(
            (
                (cell_hbm, cell), (cell_pin_hbm, slot_cell), (net_pin_hbm, net_pin),
                (count_hbm, count), (net_hbm, net), (grad_hbm, grad), (w1_hbm, w1), (w2_hbm, w2),
            )
        )
    ]
    for load in loads:
        load.start()

    barrier = pltpu.get_barrier_semaphore()

    def greet_dom(k, carry):
        pl.semaphore_signal(
            barrier, inc=1, device_id=(bat, lax.rem(me + k, owners)), device_id_type=MESH
        )
        return carry

    def greet_batch(k, carry):
        pl.semaphore_signal(
            barrier, inc=1, device_id=(lax.rem(bat + k, batches), me), device_id_type=MESH
        )
        return carry

    lax.fori_loop(1, owners, greet_dom, 0)
    lax.fori_loop(1, batches, greet_batch, 0)

    for load in loads[:4]:
        load.wait()
    cell_t[...] = cell[...].T
    cap = code.shape[2]
    lane = lax.broadcasted_iota(jnp.int32, (8, cap), 1)

    def cell_hot(to):
        return one_hot_t(slot_cell[pl.ds(to, 1), :], cells)

    def net_code(to, carry):
        code[to] = jnp.where(lane < count[0, to], net_pin[pl.ds(to, 1), :], -1)
        return carry

    lax.fori_loop(0, owners, net_code, 0)
    code_recv[me] = code[me]
    recv[me] = mm(cell_t[...], cell_hot(me)).astype(BF)

    pl.semaphore_wait(barrier, owners + batches - 2)

    def code_copy(to, frm):
        return pltpu.make_async_remote_copy(
            src_ref=code.at[to], dst_ref=code_recv.at[frm],
            send_sem=code_ssem.at[to], recv_sem=code_rsem.at[frm],
            device_id=(bat, to), device_id_type=MESH,
        )

    def row_copy(to, frm):
        return pltpu.make_async_remote_copy(
            src_ref=send.at[to], dst_ref=recv.at[frm],
            send_sem=send_sem.at[to], recv_sem=recv_sem.at[frm],
            device_id=(bat, to), device_id_type=MESH,
        )

    def ret_copy(to, frm):
        return pltpu.make_async_remote_copy(
            src_ref=ret_send.at[to], dst_ref=ret_recv.at[frm],
            send_sem=ret_ssem.at[to], recv_sem=ret_rsem.at[frm],
            device_id=(bat, to), device_id_type=MESH,
        )

    def send_to(to):
        send[to] = mm(cell_t[...], cell_hot(to)).astype(BF)
        row_copy(to, me).start()

    def send_rows(j, carry):
        chip = lax.rem(zat - j + depth, depth)
        for i in range(2):
            send_to(2 * chip + i)
        return carry

    def send_codes(k, carry):
        code_copy(lax.rem(me + k, owners), me).start()
        return carry

    lax.fori_loop(1, owners, send_codes, 0)
    send_to(sibling)
    lax.fori_loop(1, depth, send_rows, 0)

    for load in loads[4:]:
        load.wait()
    net_t[0:feat, :] = net[...].T
    net_t[feat:, :] = grad[...].T
    w1_t[...] = w1[...].T
    total[...] = jnp.zeros_like(total)

    def early(j, carry):
        chip = lax.rem(zat + j, depth)
        for i in range(2):
            src = 2 * chip + i

            @pl.when(src != me)
            def _():
                code_copy(src, src).wait_recv()

            hot_all[j, :, i * cap : (i + 1) * cap] = one_hot_t(code_recv[src, 0:1, :], nets)
        rows = mm(net_t[...], hot_all[j]).astype(BF)
        net_all[j] = rows[0:feat, :]
        grad_all[j] = rows[feat:, :]
        pre_all[j] = mm(w1_t[:, feat:], net_all[j])
        hid_grad_all[j] = mm(w2[...], grad_all[j])
        return carry

    lax.fori_loop(0, depth, early, 0)

    def late(j, carry):
        chip = lax.rem(zat + j, depth)
        for i in range(2):
            src = 2 * chip + i

            @pl.when(src != me)
            def _():
                row_copy(src, src).wait_recv()

            cell_all[j, :, i * cap : (i + 1) * cap] = recv[src]
        pre = pre_all[j] + mm(w1_t[:, 0:feat], cell_all[j])
        sig = 0.5 + 0.5 * jnp.tanh(0.5 * pre)
        hidden = (pre * sig).astype(BF)
        pre_grad = (hid_grad_all[j] * sig * (1.0 + pre * (1.0 - sig))).astype(BF)
        pre_grad_all[j] = pre_grad
        back = mm(w1[0:feat, :], pre_grad).astype(BF)
        for i in range(2):
            src = 2 * chip + i
            ret_send[src] = back[:, i * cap : (i + 1) * cap]

            @pl.when(src != me)
            def _():
                ret_copy(src, me).start()

        total[0:feat, 0:mid] += mm_t(cell_all[j], pre_grad)
        total[feat:, 0:mid] += mm_t(net_all[j], pre_grad)
        total[:, mid:] += mm_t(hidden, grad_all[j])
        return carry

    lax.fori_loop(0, depth, late, 0)

    rows_b = part_bat.shape[0]

    def own_rows(side, piece):
        start = pl.multiple_of(side * half + piece * rows_b, rows_b)
        return total[pl.ds(start, rows_b), :]

    def core_copy(piece):
        return pltpu.make_async_remote_copy(
            src_ref=core_send.at[piece], dst_ref=core_recv.at[piece],
            send_sem=core_ssem.at[piece], recv_sem=core_rsem.at[piece],
            device_id=(bat, sibling), device_id_type=MESH,
        )

    def core_go(k, carry):
        piece = lax.rem(bat + k, batches)
        core_send[piece] = own_rows(1 - core, piece).astype(BF)
        core_copy(piece).start()
        return carry

    lax.fori_loop(1, batches + 1, core_go, 0)
    net_out[...] = jnp.zeros_like(net_out)

    def net_side(j, carry):
        back = mm(w1[feat:, :], pre_grad_all[j]).astype(BF)
        net_out[...] += mm_t(hot_all[j], back)
        return carry

    lax.fori_loop(0, depth, net_side, 0)

    def bat_copy(to, frm):
        return pltpu.make_async_remote_copy(
            src_ref=bat_send.at[to], dst_ref=bat_recv.at[frm],
            send_sem=bat_ssem.at[to], recv_sem=bat_rsem.at[frm],
            device_id=(to, me), device_id_type=MESH,
        )

    def bat_go(k, carry):
        to = lax.rem(bat + k, batches)
        core_copy(to).wait_recv()
        bat_send[to] = (own_rows(core, to) + core_recv[to].astype(F32)).astype(BF)
        bat_copy(to, bat).start()
        return carry

    lax.fori_loop(1, batches, bat_go, 0)
    core_copy(bat).wait_recv()
    part_bat[...] = own_rows(core, bat) + core_recv[bat].astype(F32)

    def bat_add(k, carry):
        frm = lax.rem(bat - k + batches, batches)
        bat_copy(frm, frm).wait_recv()
        part_bat[...] += bat_recv[frm].astype(F32)
        return carry

    lax.fori_loop(1, batches, bat_add, 0)
    split_z = z_send.shape[0] > 1
    z_send[...] = part_bat[...].astype(BF).reshape(z_send.shape)

    def z_copy(to, frm):
        return pltpu.make_async_remote_copy(
            src_ref=z_send.at[to if split_z else 0], dst_ref=z_recv.at[frm],
            send_sem=z_ssem.at[to], recv_sem=z_rsem.at[frm],
            device_id=(bat, 2 * to + core), device_id_type=MESH,
        )

    def z_go(k, carry):
        z_copy(lax.rem(zat + k, depth), zat).start()
        return carry

    lax.fori_loop(1, depth, z_go, 0)
    z_recv[zat] = z_send[zat if split_z else 0]

    def z_wait(k, carry):
        frm = lax.rem(zat - k + depth, depth)
        z_copy(frm, frm).wait_recv()
        return carry

    lax.fori_loop(1, depth, z_wait, 0)
    summed = z_recv[0].astype(F32)
    for other in range(1, depth):
        summed += z_recv[other].astype(F32)
    summed = summed.astype(BF)

    def gz_copy(to, frm):
        spot = full.at[core, bat, pl.ds(frm * rows_z, rows_z), :]
        return pltpu.make_async_remote_copy(
            src_ref=spot, dst_ref=spot,
            send_sem=gz_ssem.at[to], recv_sem=gz_rsem.at[frm],
            device_id=(bat, 2 * to + core), device_id_type=MESH,
        )

    def gz_go(k, carry):
        gz_copy(lax.rem(zat + k, depth), zat).start()
        return carry

    def gz_wait(k, carry):
        frm = lax.rem(zat - k + depth, depth)
        gz_copy(frm, frm).wait_recv()
        return carry

    if split_z:
        full[core, bat, pl.ds(pl.multiple_of(zat * rows_z, rows_z), rows_z), :] = summed
        lax.fori_loop(1, depth, gz_go, 0)
        lax.fori_loop(1, depth, gz_wait, 0)
    else:
        full[core, bat] = summed

    def gbat_copy(to, frm):
        return pltpu.make_async_remote_copy(
            src_ref=full.at[core, frm], dst_ref=full.at[core, frm],
            send_sem=gbat_ssem.at[to], recv_sem=gbat_rsem.at[frm],
            device_id=(to, me), device_id_type=MESH,
        )

    def gbat_go(k, carry):
        gbat_copy(lax.rem(bat + k, batches), bat).start()
        return carry

    def gcore_copy(side, piece):
        return pltpu.make_async_remote_copy(
            src_ref=full.at[side, piece], dst_ref=full.at[side, piece],
            send_sem=gcore_ssem.at[piece], recv_sem=gcore_rsem.at[piece],
            device_id=(bat, sibling), device_id_type=MESH,
        )

    def gbat_wait(k, carry):
        frm = lax.rem(bat - k + batches, batches)
        gbat_copy(frm, frm).wait_recv()
        gcore_copy(core, frm).start()
        return carry

    lax.fori_loop(1, batches, gbat_go, 0)
    gcore_copy(core, bat).start()
    lax.fori_loop(1, batches, gbat_wait, 0)

    cell_out[...] = mm_t(cell_hot(me), ret_send[me])

    def gather_back(k, carry):
        frm = lax.rem(me + k, owners)
        ret_copy(frm, frm).wait_recv()
        cell_out[...] += mm_t(cell_hot(frm), ret_recv[frm])
        return carry

    lax.fori_loop(1, owners, gather_back, 0)

    def gcore_wait(piece, carry):
        gcore_copy(1 - core, piece).wait_recv()
        return carry

    lax.fori_loop(0, batches, gcore_wait, 0)

    def drain_dom(k, carry):
        to = lax.rem(me + k, owners)
        code_copy(to, me).wait_send()
        row_copy(to, me).wait_send()
        ret_copy(to, me).wait_send()
        return carry

    def drain_batch(k, carry):
        to = lax.rem(bat + k, batches)
        bat_copy(to, bat).wait_send()
        gbat_copy(to, bat).wait_send()
        return carry

    def drain_z(k, carry):
        to = lax.rem(zat + k, depth)
        z_copy(to, zat).wait_send()
        if split_z:
            gz_copy(to, zat).wait_send()
        return carry

    lax.fori_loop(1, owners, drain_dom, 0)
    lax.fori_loop(1, batches, drain_batch, 0)
    lax.fori_loop(1, depth, drain_z, 0)

    def drain_core(piece, carry):
        core_copy(piece).wait_send()
        gcore_copy(core, piece).wait_send()
        return carry

    lax.fori_loop(0, batches, drain_core, 0)


def finish(scale, cell_sum, net_sum, full, cell_out, net_out, first, second):
    mid = first.shape[1]
    cell_out[...] = cell_sum[...]
    net_out[...] = net_sum[...]
    first[...] = full[:, 0:mid].astype(F32) * scale
    second[...] = full[:, mid:].astype(F32) * scale


def on_device(cell_feat, net_feat, net_grad, w_first, w_second, pin_cell, pin_net, pin_count):
    owners = lax.axis_size("dom")
    batches = lax.axis_size("batch")
    cell, net, grad = cell_feat[0], net_feat[0], net_grad[0]
    capacity = pin_cell.shape[3]
    cells, feat = cell.shape
    nets = net.shape[0]
    fan_in, mid = w_first.shape
    width = mid + feat
    depth = owners // 2
    scale = 1.0 / math.sqrt(batches * owners * owners * capacity)
    half = fan_in // 2
    rows_b = half // batches
    split_z = rows_b // depth >= 16
    rows_z = rows_b // depth if split_z else rows_b
    parts_z = depth if split_z else 1
    dma = pltpu.SemaphoreType.DMA
    vmem = pltpu.VMEM
    hbm = pl.BlockSpec(memory_space=pltpu.HBM)
    on_chip = pl.BlockSpec(memory_space=pltpu.VMEM)

    def block(rows, columns):
        return pl.BlockSpec((rows // 4, columns), lambda i: (i, 0))

    cell_sum, net_sum, full = pl.pallas_call(
        functools.partial(kernel, batches, owners, rows_z),
        out_shape=(
            jax.ShapeDtypeStruct((cells, feat), F32),
            jax.ShapeDtypeStruct((nets, feat), F32),
            jax.ShapeDtypeStruct((2, batches, rows_b, width), BF),
        ),
        in_specs=[hbm] * 8,
        out_specs=[on_chip] * 3,
        scratch_shapes=[
            vmem((cells, feat), BF),
            vmem((nets, feat), BF),
            vmem((nets, feat), BF),
            vmem((fan_in, mid), BF),
            vmem((mid, feat), BF),
            vmem((owners, capacity), jnp.int32),
            vmem((owners, capacity), jnp.int32),
            pltpu.SMEM((1, owners), jnp.int32),
            vmem((owners, 8, capacity), jnp.int32),
            vmem((feat, cells), BF),
            vmem((2 * feat, nets), BF),
            vmem((mid, fan_in), BF),
            vmem((depth, feat, 2 * capacity), BF),
            vmem((depth, feat, 2 * capacity), BF),
            vmem((depth, feat, 2 * capacity), BF),
            vmem((depth, nets, 2 * capacity), BF),
            vmem((depth, mid, 2 * capacity), F32),
            vmem((depth, mid, 2 * capacity), F32),
            vmem((depth, mid, 2 * capacity), BF),
            vmem((fan_in, width), F32),
            vmem((owners, feat, capacity), BF),
            vmem((owners, feat, capacity), BF),
            vmem((owners, 8, capacity), jnp.int32),
            vmem((owners, feat, capacity), BF),
            vmem((owners, feat, capacity), BF),
            vmem((batches, rows_b, width), BF),
            vmem((batches, rows_b, width), BF),
            vmem((batches, rows_b, width), BF),
            vmem((batches, rows_b, width), BF),
            vmem((rows_b, width), F32),
            vmem((parts_z, rows_z, width), BF),
            vmem((depth, rows_z, width), BF),
            dma((8,)),
            dma((owners,)), dma((owners,)), dma((owners,)), dma((owners,)),
            dma((owners,)), dma((owners,)),
            dma((batches,)), dma((batches,)), dma((batches,)), dma((batches,)), dma((depth,)), dma((depth,)),
            dma((batches,)), dma((batches,)), dma((batches,)), dma((batches,)), dma((depth,)), dma((depth,)),
        ],
        compiler_params=pltpu.CompilerParams(
            collective_id=0, has_side_effects=True, vmem_limit_bytes=60 * 1024 * 1024
        ),
    )(cell, net, grad, w_first, w_second, pin_cell[0, 0], pin_net[0, 0], pin_count[0])
    cell_out, net_out, first, second = pl.pallas_call(
        functools.partial(finish, scale),
        out_shape=(
            jax.ShapeDtypeStruct((cells, feat), F32),
            jax.ShapeDtypeStruct((nets, feat), F32),
            jax.ShapeDtypeStruct((fan_in, mid), F32),
            jax.ShapeDtypeStruct((mid, feat), F32),
        ),
        grid=(4,),
        in_specs=[block(cells, feat), block(nets, feat), block(fan_in, width)],
        out_specs=[block(cells, feat), block(nets, feat), block(fan_in, mid), block(mid, feat)],
    )(cell_sum, net_sum, full.reshape(fan_in, width))
    return (cell_out[None], net_out[None], first, second)


def solution(mesh):
    return jax.shard_map(
        on_device,
        mesh=mesh,
        in_specs=(
            P("batch", "dom", None),
            P("batch", "dom", None),
            P("batch", "dom", None),
            P(),
            P(),
            P("batch", "dom", None, None),
            P("batch", "dom", None, None),
            P("batch", "dom", None),
        ),
        out_specs=(P("batch", "dom", None), P("batch", "dom", None), P(), P()),
        check_vma=False,
    )
```

```python
import functools
import math

import jax
import jax.numpy as jnp
from jax import lax
from jax.experimental import pallas as pl
from jax.experimental.pallas import tpu as pltpu
from jax.sharding import PartitionSpec as P

BF = jnp.bfloat16
F32 = jnp.float32
MESH = pl.DeviceIdType.MESH


def mm(a, b):
    return jnp.dot(a, b, preferred_element_type=F32)


def mm_t(a, b):
    return lax.dot_general(a, b, (((1,), (1,)), ((), ())), preferred_element_type=F32)


def one_hot_t(row, count):
    at = lax.broadcasted_iota(jnp.int32, (count, row.shape[1]), 0)
    return jnp.where(at == row, 1.0, 0.0).astype(BF)


def kernel(
    batches, owners, rows_z,
    cell_hbm, net_hbm, grad_hbm, w1_hbm, w2_hbm, cell_pin_hbm, net_pin_hbm, count_hbm,
    cell_out, net_out, full,
    cell, net, grad, w1, w2, slot_cell, net_pin, count, code,
    cell_t, net_t, w1_t, cell_all, net_all, grad_all, hot_all, pre_all, hid_grad_all, pre_grad_all, total,
    send, recv, code_recv, ret_send, ret_recv,
    core_send, core_recv, bat_send, bat_recv, part_bat, z_send, z_recv,
    load_sem,
    send_sem, recv_sem, code_ssem, code_rsem, ret_ssem, ret_rsem,
    core_ssem, core_rsem, bat_ssem, bat_rsem, z_ssem, z_rsem, gcore_ssem, gcore_rsem, gbat_ssem, gbat_rsem, gz_ssem, gz_rsem,
):
    bat = lax.axis_index("batch")
    me = lax.axis_index("dom")
    feat = cell.shape[1]
    cells = cell.shape[0]
    nets = net.shape[0]
    mid = w1.shape[1]
    core = lax.rem(me, 2)
    depth = owners // 2
    zat = me // 2
    sibling = me + 1 - 2 * core
    half = total.shape[0] // 2

    loads = [
        pltpu.make_async_copy(a, b, load_sem.at[i])
        for i, (a, b) in enumerate(
            (
                (cell_hbm, cell), (cell_pin_hbm, slot_cell), (net_pin_hbm, net_pin),
                (count_hbm, count), (net_hbm, net), (grad_hbm, grad), (w1_hbm, w1), (w2_hbm, w2),
            )
        )
    ]
    for load in loads:
        load.start()

    barrier = pltpu.get_barrier_semaphore()

    def greet_dom(k, carry):
        pl.semaphore_signal(
            barrier, inc=1, device_id=(bat, lax.rem(me + k, owners)), device_id_type=MESH
        )
        return carry

    def greet_batch(k, carry):
        pl.semaphore_signal(
            barrier, inc=1, device_id=(lax.rem(bat + k, batches), me), device_id_type=MESH
        )
        return carry

    lax.fori_loop(1, owners, greet_dom, 0)
    lax.fori_loop(1, batches, greet_batch, 0)

    for load in loads[:4]:
        load.wait()
    cell_t[...] = cell[...].T
    cap = code.shape[2]
    lane = lax.broadcasted_iota(jnp.int32, (8, cap), 1)

    def cell_hot(to):
        return one_hot_t(slot_cell[pl.ds(to, 1), :], cells)

    def net_code(to, carry):
        code[to] = jnp.where(lane < count[0, to], net_pin[pl.ds(to, 1), :], -1)
        return carry

    lax.fori_loop(0, owners, net_code, 0)
    code_recv[me] = code[me]
    recv[me] = mm(cell_t[...], cell_hot(me)).astype(BF)

    pl.semaphore_wait(barrier, owners + batches - 2)

    def code_copy(to, frm):
        return pltpu.make_async_remote_copy(
            src_ref=code.at[to], dst_ref=code_recv.at[frm],
            send_sem=code_ssem.at[to], recv_sem=code_rsem.at[frm],
            device_id=(bat, to), device_id_type=MESH,
        )

    def row_copy(to, frm):
        return pltpu.make_async_remote_copy(
            src_ref=send.at[to], dst_ref=recv.at[frm],
            send_sem=send_sem.at[to], recv_sem=recv_sem.at[frm],
            device_id=(bat, to), device_id_type=MESH,
        )

    def ret_copy(to, frm):
        return pltpu.make_async_remote_copy(
            src_ref=ret_send.at[to], dst_ref=ret_recv.at[frm],
            send_sem=ret_ssem.at[to], recv_sem=ret_rsem.at[frm],
            device_id=(bat, to), device_id_type=MESH,
        )

    def send_to(to):
        send[to] = mm(cell_t[...], cell_hot(to)).astype(BF)
        row_copy(to, me).start()

    def send_rows(j, carry):
        chip = lax.rem(zat - j + depth, depth)
        for i in range(2):
            send_to(2 * chip + i)
        return carry

    def send_codes(k, carry):
        code_copy(lax.rem(me + k, owners), me).start()
        return carry

    lax.fori_loop(1, owners, send_codes, 0)
    send_to(sibling)
    lax.fori_loop(1, depth, send_rows, 0)

    for load in loads[4:]:
        load.wait()
    net_t[0:feat, :] = net[...].T
    net_t[feat:, :] = grad[...].T
    w1_t[...] = w1[...].T
    total[...] = jnp.zeros_like(total)

    def early(j, carry):
        chip = lax.rem(zat + j, depth)
        for i in range(2):
            src = 2 * chip + i

            @pl.when(src != me)
            def _():
                code_copy(src, src).wait_recv()

            hot_all[j, :, i * cap : (i + 1) * cap] = one_hot_t(code_recv[src, 0:1, :], nets)
        rows = mm(net_t[...], hot_all[j]).astype(BF)
        net_all[j] = rows[0:feat, :]
        grad_all[j] = rows[feat:, :]
        pre_all[j] = mm(w1_t[:, feat:], net_all[j])
        hid_grad_all[j] = mm(w2[...], grad_all[j])
        return carry

    lax.fori_loop(0, depth, early, 0)

    def late(j, carry):
        chip = lax.rem(zat + j, depth)
        for i in range(2):
            src = 2 * chip + i

            @pl.when(src != me)
            def _():
                row_copy(src, src).wait_recv()

            cell_all[j, :, i * cap : (i + 1) * cap] = recv[src]
        pre = pre_all[j] + mm(w1_t[:, 0:feat], cell_all[j])
        sig = 0.5 + 0.5 * jnp.tanh(0.5 * pre)
        hidden = (pre * sig).astype(BF)
        pre_grad = (hid_grad_all[j] * sig * (1.0 + pre * (1.0 - sig))).astype(BF)
        pre_grad_all[j] = pre_grad
        back = mm(w1[0:feat, :], pre_grad).astype(BF)
        for i in range(2):
            src = 2 * chip + i
            ret_send[src] = back[:, i * cap : (i + 1) * cap]

            @pl.when(src != me)
            def _():
                ret_copy(src, me).start()

        total[0:feat, 0:mid] += mm_t(cell_all[j], pre_grad)
        total[feat:, 0:mid] += mm_t(net_all[j], pre_grad)
        total[:, mid:] += mm_t(hidden, grad_all[j])
        return carry

    lax.fori_loop(0, depth, late, 0)

    rows_b = part_bat.shape[0]

    def own_rows(side, piece):
        start = pl.multiple_of(side * half + piece * rows_b, rows_b)
        return total[pl.ds(start, rows_b), :]

    def core_copy(piece):
        return pltpu.make_async_remote_copy(
            src_ref=core_send.at[piece], dst_ref=core_recv.at[piece],
            send_sem=core_ssem.at[piece], recv_sem=core_rsem.at[piece],
            device_id=(bat, sibling), device_id_type=MESH,
        )

    def core_go(k, carry):
        piece = lax.rem(bat + k, batches)
        core_send[piece] = own_rows(1 - core, piece).astype(BF)
        core_copy(piece).start()
        return carry

    lax.fori_loop(1, batches + 1, core_go, 0)
    net_out[...] = jnp.zeros_like(net_out)

    def net_side(j, carry):
        back = mm(w1[feat:, :], pre_grad_all[j]).astype(BF)
        net_out[...] += mm_t(hot_all[j], back)
        return carry

    lax.fori_loop(0, depth, net_side, 0)

    def bat_copy(to, frm):
        return pltpu.make_async_remote_copy(
            src_ref=bat_send.at[to], dst_ref=bat_recv.at[frm],
            send_sem=bat_ssem.at[to], recv_sem=bat_rsem.at[frm],
            device_id=(to, me), device_id_type=MESH,
        )

    def bat_go(k, carry):
        to = lax.rem(bat + k, batches)
        core_copy(to).wait_recv()
        bat_send[to] = (own_rows(core, to) + core_recv[to].astype(F32)).astype(BF)
        bat_copy(to, bat).start()
        return carry

    lax.fori_loop(1, batches, bat_go, 0)
    core_copy(bat).wait_recv()
    part_bat[...] = own_rows(core, bat) + core_recv[bat].astype(F32)

    def bat_add(k, carry):
        frm = lax.rem(bat - k + batches, batches)
        bat_copy(frm, frm).wait_recv()
        part_bat[...] += bat_recv[frm].astype(F32)
        return carry

    lax.fori_loop(1, batches, bat_add, 0)
    split_z = z_send.shape[0] > 1
    z_send[...] = part_bat[...].astype(BF).reshape(z_send.shape)

    def z_copy(to, frm):
        return pltpu.make_async_remote_copy(
            src_ref=z_send.at[to if split_z else 0], dst_ref=z_recv.at[frm],
            send_sem=z_ssem.at[to], recv_sem=z_rsem.at[frm],
            device_id=(bat, 2 * to + core), device_id_type=MESH,
        )

    def z_go(k, carry):
        z_copy(lax.rem(zat + k, depth), zat).start()
        return carry

    lax.fori_loop(1, depth, z_go, 0)
    z_recv[zat] = z_send[zat if split_z else 0]

    def z_wait(k, carry):
        frm = lax.rem(zat - k + depth, depth)
        z_copy(frm, frm).wait_recv()
        return carry

    lax.fori_loop(1, depth, z_wait, 0)
    summed = z_recv[0].astype(F32)
    for other in range(1, depth):
        summed += z_recv[other].astype(F32)
    summed = summed.astype(BF)

    def gz_copy(to, frm):
        spot = full.at[core, bat, pl.ds(frm * rows_z, rows_z), :]
        return pltpu.make_async_remote_copy(
            src_ref=spot, dst_ref=spot,
            send_sem=gz_ssem.at[to], recv_sem=gz_rsem.at[frm],
            device_id=(bat, 2 * to + core), device_id_type=MESH,
        )

    def gz_go(k, carry):
        gz_copy(lax.rem(zat + k, depth), zat).start()
        return carry

    def gz_wait(k, carry):
        frm = lax.rem(zat - k + depth, depth)
        gz_copy(frm, frm).wait_recv()
        return carry

    if split_z:
        full[core, bat, pl.ds(pl.multiple_of(zat * rows_z, rows_z), rows_z), :] = summed
        lax.fori_loop(1, depth, gz_go, 0)
        lax.fori_loop(1, depth, gz_wait, 0)
    else:
        full[core, bat] = summed

    def gbat_copy(to, frm):
        return pltpu.make_async_remote_copy(
            src_ref=full.at[core, frm], dst_ref=full.at[core, frm],
            send_sem=gbat_ssem.at[to], recv_sem=gbat_rsem.at[frm],
            device_id=(to, me), device_id_type=MESH,
        )

    def gbat_go(k, carry):
        gbat_copy(lax.rem(bat + k, batches), bat).start()
        return carry

    def gcore_copy(side, piece):
        return pltpu.make_async_remote_copy(
            src_ref=full.at[side, piece], dst_ref=full.at[side, piece],
            send_sem=gcore_ssem.at[piece], recv_sem=gcore_rsem.at[piece],
            device_id=(bat, sibling), device_id_type=MESH,
        )

    def gbat_wait(k, carry):
        frm = lax.rem(bat - k + batches, batches)
        gbat_copy(frm, frm).wait_recv()
        gcore_copy(core, frm).start()
        return carry

    lax.fori_loop(1, batches, gbat_go, 0)
    gcore_copy(core, bat).start()
    lax.fori_loop(1, batches, gbat_wait, 0)

    cell_out[...] = mm_t(cell_hot(me), ret_send[me])

    def gather_back(k, carry):
        frm = lax.rem(me + k, owners)
        ret_copy(frm, frm).wait_recv()
        cell_out[...] += mm_t(cell_hot(frm), ret_recv[frm])
        return carry

    lax.fori_loop(1, owners, gather_back, 0)

    def gcore_wait(piece, carry):
        gcore_copy(1 - core, piece).wait_recv()
        return carry

    lax.fori_loop(0, batches, gcore_wait, 0)

    def drain_dom(k, carry):
        to = lax.rem(me + k, owners)
        code_copy(to, me).wait_send()
        row_copy(to, me).wait_send()
        ret_copy(to, me).wait_send()
        return carry

    def drain_batch(k, carry):
        to = lax.rem(bat + k, batches)
        bat_copy(to, bat).wait_send()
        gbat_copy(to, bat).wait_send()
        return carry

    def drain_z(k, carry):
        to = lax.rem(zat + k, depth)
        z_copy(to, zat).wait_send()
        if split_z:
            gz_copy(to, zat).wait_send()
        return carry

    lax.fori_loop(1, owners, drain_dom, 0)
    lax.fori_loop(1, batches, drain_batch, 0)
    lax.fori_loop(1, depth, drain_z, 0)

    def drain_core(piece, carry):
        core_copy(piece).wait_send()
        gcore_copy(core, piece).wait_send()
        return carry

    lax.fori_loop(0, batches, drain_core, 0)


def finish(scale, cell_sum, net_sum, full, cell_out, net_out, first, second):
    mid = first.shape[1]
    cell_out[...] = cell_sum[...]
    net_out[...] = net_sum[...]
    first[...] = full[:, 0:mid].astype(F32) * scale
    second[...] = full[:, mid:].astype(F32) * scale


def on_device(cell_feat, net_feat, net_grad, w_first, w_second, pin_cell, pin_net, pin_count):
    owners = lax.axis_size("dom")
    batches = lax.axis_size("batch")
    cell, net, grad = cell_feat[0], net_feat[0], net_grad[0]
    capacity = pin_cell.shape[3]
    cells, feat = cell.shape
    nets = net.shape[0]
    fan_in, mid = w_first.shape
    width = mid + feat
    depth = owners // 2
    scale = 1.0 / math.sqrt(batches * owners * owners * capacity)
    half = fan_in // 2
    rows_b = half // batches
    split_z = rows_b // depth >= 16
    rows_z = rows_b // depth if split_z else rows_b
    parts_z = depth if split_z else 1
    dma = pltpu.SemaphoreType.DMA
    vmem = pltpu.VMEM
    hbm = pl.BlockSpec(memory_space=pltpu.HBM)
    on_chip = pl.BlockSpec(memory_space=pltpu.VMEM)

    def block(rows, columns):
        return pl.BlockSpec((rows // 2, columns), lambda i: (i, 0))

    cell_sum, net_sum, full = pl.pallas_call(
        functools.partial(kernel, batches, owners, rows_z),
        out_shape=(
            jax.ShapeDtypeStruct((cells, feat), F32),
            jax.ShapeDtypeStruct((nets, feat), F32),
            jax.ShapeDtypeStruct((2, batches, rows_b, width), BF),
        ),
        in_specs=[hbm] * 8,
        out_specs=[on_chip] * 3,
        scratch_shapes=[
            vmem((cells, feat), BF),
            vmem((nets, feat), BF),
            vmem((nets, feat), BF),
            vmem((fan_in, mid), BF),
            vmem((mid, feat), BF),
            vmem((owners, capacity), jnp.int32),
            vmem((owners, capacity), jnp.int32),
            pltpu.SMEM((1, owners), jnp.int32),
            vmem((owners, 8, capacity), jnp.int32),
            vmem((feat, cells), BF),
            vmem((2 * feat, nets), BF),
            vmem((mid, fan_in), BF),
            vmem((depth, feat, 2 * capacity), BF),
            vmem((depth, feat, 2 * capacity), BF),
            vmem((depth, feat, 2 * capacity), BF),
            vmem((depth, nets, 2 * capacity), BF),
            vmem((depth, mid, 2 * capacity), F32),
            vmem((depth, mid, 2 * capacity), F32),
            vmem((depth, mid, 2 * capacity), BF),
            vmem((fan_in, width), F32),
            vmem((owners, feat, capacity), BF),
            vmem((owners, feat, capacity), BF),
            vmem((owners, 8, capacity), jnp.int32),
            vmem((owners, feat, capacity), BF),
            vmem((owners, feat, capacity), BF),
            vmem((batches, rows_b, width), BF),
            vmem((batches, rows_b, width), BF),
            vmem((batches, rows_b, width), BF),
            vmem((batches, rows_b, width), BF),
            vmem((rows_b, width), F32),
            vmem((parts_z, rows_z, width), BF),
            vmem((depth, rows_z, width), BF),
            dma((8,)),
            dma((owners,)), dma((owners,)), dma((owners,)), dma((owners,)),
            dma((owners,)), dma((owners,)),
            dma((batches,)), dma((batches,)), dma((batches,)), dma((batches,)), dma((depth,)), dma((depth,)),
            dma((batches,)), dma((batches,)), dma((batches,)), dma((batches,)), dma((depth,)), dma((depth,)),
        ],
        compiler_params=pltpu.CompilerParams(
            collective_id=0, has_side_effects=True, vmem_limit_bytes=60 * 1024 * 1024
        ),
    )(cell, net, grad, w_first, w_second, pin_cell[0, 0], pin_net[0, 0], pin_count[0])
    cell_out, net_out, first, second = pl.pallas_call(
        functools.partial(finish, scale),
        out_shape=(
            jax.ShapeDtypeStruct((cells, feat), F32),
            jax.ShapeDtypeStruct((nets, feat), F32),
            jax.ShapeDtypeStruct((fan_in, mid), F32),
            jax.ShapeDtypeStruct((mid, feat), F32),
        ),
        grid=(2,),
        in_specs=[block(cells, feat), block(nets, feat), block(fan_in, width)],
        out_specs=[block(cells, feat), block(nets, feat), block(fan_in, mid), block(mid, feat)],
    )(cell_sum, net_sum, full.reshape(fan_in, width))
    return (cell_out[None], net_out[None], first, second)


def solution(mesh):
    return jax.shard_map(
        on_device,
        mesh=mesh,
        in_specs=(
            P("batch", "dom", None),
            P("batch", "dom", None),
            P("batch", "dom", None),
            P(),
            P(),
            P("batch", "dom", None, None),
            P("batch", "dom", None, None),
            P("batch", "dom", None),
        ),
        out_specs=(P("batch", "dom", None), P("batch", "dom", None), P(), P()),
        check_vma=False,
    )
```
